128 devices in a mesh: clique: 2 (over core), dp: 4 (over z), hst: 16 (over y, x).
Axes of the slice: x: 4, y: 4, z: 4, core: 2. Of those that a mesh axis runs over, the one named last changes fastest.
Arguments:
- hot_table: bfloat16 [4096, 1024], P('clique'), may hold values from -6 to 6
- cold_table: bfloat16 [32768, 1024], P('hst'), may hold values from -6 to 6
- seed_source: int32 [128, 64], P(('clique', 'dp', 'hst')), may hold values from 0 to 8191, as said below
- hop1_source: int32 [128, 640], P(('clique', 'dp', 'hst')), may hold values from 0 to 8191, as said below
- hop2_source: int32 [128, 9600], P(('clique', 'dp', 'hst')), may hold values from 0 to 8191, as said below
- cold_ask: int32 [128, 16, 256], P(('clique', 'dp', 'hst')), may hold values from 0 to 2047, as said below
- cotangent: bfloat16 [8192, 1024], P(('clique', 'dp', 'hst')), may hold values from -0.06591797 to 0.06591797
- w1_self: bfloat16 [1024, 1024], replicated, may hold values from -0.1875 to 0.1875
- w1_neigh: bfloat16 [1024, 1024], replicated, may hold values from -0.1875 to 0.1875
- w2_self: bfloat16 [1024, 1024], replicated, may hold values from -0.1875 to 0.1875
- w2_neigh: bfloat16 [1024, 1024], replicated, may hold values from -0.1875 to 0.1875
Outputs:
- embedding: bfloat16 [8192, 1024], P(('clique', 'dp', 'hst'))
- grad_w1_self: float32 [1024, 1024], P(('clique', 'hst'))
- grad_w1_neigh: float32 [1024, 1024], P(('clique', 'hst'))
- grad_w2_self: float32 [1024, 1024], P(('clique', 'hst'))
- grad_w2_neigh: float32 [1024, 1024], P(('clique', 'hst'))
The draws below stay inside these ranges and needn't reach their ends.
Inputs may be any that keep to these rules, and one draw needn't show every extreme that they name: `seed_source`: values below 4096 name a hot cache row; a value 4096 + o * 256 + s names slot s of this device's request to cold owner o. Every slot of every owner is named by at least one node of the device's tree (seed, first-hop or second-hop). `hop1_source`: as for seed_source. `hop2_source`: as for seed_source. `cold_ask`: each entry is a row within the owner's block of cold_table.
All inputs are finite; a program needn't handle non-finite values.
Results may differ from the reference program's by a relative error of at most 0.0044.
The reference program's roundings to bfloat16 on the way (of `level_mean`, `hidden`, `hidden_mean` and `grad_pre`) count: a program that leaves them out, or rounds other values in their place, can miss the bound.
Values may be sent and summed in bfloat16 or wider, within the bound.
No kernel may reach another device: no remote copies, remote signals or barrier semaphores. Data moves between devices by JAX's collectives and lax.ppermute only.
A program may use at most 128 MiB of HBM per device.

```python
import jax
import jax.numpy as jnp
from jax import lax

F = 1024
H = 1024
K2 = 10
K1 = 15
SEEDS = 64
HOT = 4096
COLD_DEV = 2048
CAP = 256
OWNERS = 16
WORKERS = 128
ALL_SEEDS = 8192
HOP1 = 640
COLD_ROWS = 32768


def sampled_tree(key):
    key = jax.random.fold_in(key, 7301)
    subkeys = jax.random.split(key, 8)
    requests = jax.random.randint(subkeys[3], (WORKERS, OWNERS, CAP), 0, COLD_DEV)
    node_total = SEEDS * (1 + K2 + K2 * K1)
    slots_total = OWNERS * CAP
    ranks = jnp.arange(node_total)[None, :]
    spare_cold = HOT + jax.random.randint(subkeys[4], (WORKERS, node_total), 0, slots_total)
    hot_source = jax.random.randint(subkeys[5], (WORKERS, node_total), 0, HOT)
    picker = jax.random.randint(subkeys[6], (WORKERS, node_total), 0, 2)
    by_rank = jnp.where(picker == 1, spare_cold, hot_source)
    by_rank = jnp.where(ranks < slots_total, HOT + jnp.minimum(ranks, slots_total - 1), by_rank)
    worker_keys = jax.random.split(subkeys[7], WORKERS)
    orders = jax.vmap(lambda k: jax.random.permutation(k, node_total))(worker_keys)
    source = jnp.take_along_axis(by_rank, orders, axis=1).astype(jnp.int32)
    return (requests.astype(jnp.int32), source)


def draw_seed_source(key, part):
    requests, source = sampled_tree(key)
    return source[:, :SEEDS]


def draw_hop1_source(key, part):
    requests, source = sampled_tree(key)
    return source[:, SEEDS:SEEDS + HOP1]


def draw_hop2_source(key, part):
    requests, source = sampled_tree(key)
    return source[:, SEEDS + HOP1:]


def draw_cold_ask(key, part):
    requests, source = sampled_tree(key)
    return requests


def level_of(rng, extent, pieces, low, largest):
    level, own = 1.0, jax.random.fold_in(rng, 6)
    for dim, shards_of in pieces:
        draws = jnp.exp(jax.random.uniform(jax.random.fold_in(own, dim), (shards_of,), jnp.float32, low / len(pieces), largest / len(pieces)))
        level = level * jnp.repeat(draws, extent[dim] // shards_of).reshape([-1 if axis == dim else 1 for axis in range(len(extent))])
    return level


def bell_draw(stream_key, dims, deviation, bound, cuts=(), held_as=jnp.bfloat16):
    array = jax.random.normal(stream_key, dims, jnp.float32) * deviation
    if len(cuts) > 0:
        array = level_of(stream_key, dims, cuts, -0.22, 0.18) * array
    return jnp.clip(array, min=-bound, max=bound).astype(held_as)


def setup_inputs(seed: int = 0) -> dict:
    arg_keys = jax.random.split(jax.random.key(seed), 12)
    hot_table = bell_draw(arg_keys[0], (HOT, F), 1.0, 6.0, ((0, 2),))
    cold_table = bell_draw(arg_keys[1], (COLD_ROWS, F), 1.0, 6.0, ((0, 16),))
    seed_source = draw_seed_source(jax.random.fold_in(arg_keys[11], 71), 0)
    hop1_source = draw_hop1_source(jax.random.fold_in(arg_keys[11], 71), 0)
    hop2_source = draw_hop2_source(jax.random.fold_in(arg_keys[11], 71), 0)
    cold_ask = draw_cold_ask(jax.random.fold_in(arg_keys[11], 71), 0)
    cotangent = bell_draw(arg_keys[6], (ALL_SEEDS, H), (ALL_SEEDS ** -0.5), 0.06591797, ((0, 128),))
    w1_self = bell_draw(arg_keys[7], (F, H), F ** -0.5, 0.1875)
    w1_neigh = bell_draw(arg_keys[8], (F, H), F ** -0.5, 0.1875)
    w2_self = bell_draw(arg_keys[9], (H, H), H ** -0.5, 0.1875)
    w2_neigh = bell_draw(arg_keys[10], (H, H), H ** -0.5, 0.1875)
    return {"hot_table": hot_table, "cold_table": cold_table, "seed_source": seed_source, "hop1_source": hop1_source, "hop2_source": hop2_source, "cold_ask": cold_ask, "cotangent": cotangent, "w1_self": w1_self, "w1_neigh": w1_neigh, "w2_self": w2_self, "w2_neigh": w2_neigh}


def fetch(source, hot_table, cold_table, requests):
    is_hot = source < HOT
    hot_pick = jnp.take(hot_table, jnp.clip(source, 0, HOT - 1).astype(jnp.int32), axis=0)
    offset = jnp.clip(source - HOT, 0, OWNERS * CAP - 1).astype(jnp.int32)
    owner = offset // CAP
    slot_index = offset % CAP
    row_index = (requests[owner, slot_index] + owner * COLD_DEV).astype(jnp.int32)
    cold_pick = jnp.take(cold_table, row_index, axis=0)
    return jnp.where(is_hot[:, None], hot_pick, cold_pick)


def mean_rows(values, fanout):
    groups = values.shape[0] // fanout
    total = jnp.sum(values.reshape(groups, fanout, values.shape[1]), axis=1, dtype=jnp.float32)
    return (total / fanout).astype(jnp.bfloat16)


def matmul(left, right):
    return jnp.dot(left, right, preferred_element_type=jnp.float32)


def inner_rows(left, right):
    return lax.dot_general(left, right, (((0,), (0,)), ((), ())), preferred_element_type=jnp.float32)


def inner_cols(left, right):
    return lax.dot_general(left, right, (((1,), (1,)), ((), ())), preferred_element_type=jnp.float32)


def reference(hot_table, cold_table, seed_source, hop1_source, hop2_source, cold_ask, cotangent, w1_self, w1_neigh, w2_self, w2_neigh):
    cot_blocks = cotangent.reshape(WORKERS, SEEDS, H)

    def one_worker(totals, items):
        seeds_src, first_src, second_src, requests, cot = items
        seed_feat = fetch(seeds_src, hot_table, cold_table, requests)
        hop1_feat = fetch(first_src, hot_table, cold_table, requests)
        hop2_feat = fetch(second_src, hot_table, cold_table, requests)
        level_in = jnp.concatenate([seed_feat, hop1_feat], 0)
        level_mean = jnp.concatenate([mean_rows(hop1_feat, K2), mean_rows(hop2_feat, K1)], 0)
        pre = matmul(level_in, w1_self) + matmul(level_mean, w1_neigh)
        hidden = jnp.maximum(pre, 0.0).astype(jnp.bfloat16)
        hidden_seed = hidden[:SEEDS]
        hidden_mean = mean_rows(hidden[SEEDS:], K2)
        embed = (matmul(hidden_seed, w2_self) + matmul(hidden_mean, w2_neigh)).astype(jnp.bfloat16)
        grad_seed = inner_cols(cot, w2_self)
        grad_mean = inner_cols(cot, w2_neigh) / K2
        grad_hop = jnp.broadcast_to(grad_mean[:, None, :], (SEEDS, K2, H)).reshape(SEEDS * K2, H)
        grad_hidden = jnp.concatenate([grad_seed, grad_hop], 0)
        grad_pre = jnp.where(pre > 0, grad_hidden, jnp.float32(0.0)).astype(jnp.bfloat16)
        terms = (inner_rows(level_in, grad_pre), inner_rows(level_mean, grad_pre),
                 inner_rows(hidden_seed, cot), inner_rows(hidden_mean, cot))
        return tuple(a + b for a, b in zip(totals, terms)), embed

    start = (jnp.zeros((F, H), jnp.float32), jnp.zeros((F, H), jnp.float32),
             jnp.zeros((H, H), jnp.float32), jnp.zeros((H, H), jnp.float32))
    totals, embeds = lax.scan(one_worker, start, (seed_source, hop1_source, hop2_source, cold_ask, cot_blocks))
    embedding = embeds.reshape(ALL_SEEDS, H)
    return (embedding, totals[0], totals[1], totals[2], totals[3])
```

```python
import functools

import jax
import jax.numpy as jnp
from jax import lax
from jax.experimental import pallas as pl
from jax.experimental.pallas import tpu as pltpu
from jax.sharding import PartitionSpec as P

K2 = 10
K1 = 15
LANES = 128
ROWS = 16
CHUNKS = 2


BF16 = jnp.bfloat16
F32 = jnp.float32


def matmul(left, right):
    return jnp.dot(left, right, preferred_element_type=F32)


def inner_rows(left, right):
    return lax.dot_general(left, right, (((0,), (0,)), ((), ())), preferred_element_type=F32)


def inner_cols(left, right):
    return lax.dot_general(left, right, (((1,), (1,)), ((), ())), preferred_element_type=F32)


def count_kernel(index_ref, *out_refs, single_blocks, block_rows, terms):
    step = pl.program_id(0)

    def fill(width):
        @pl.loop(0, block_rows // ROWS)
        def _(group):
            first = pl.multiple_of(group * ROWS, ROWS)
            index = index_ref[pl.ds(first, ROWS), :]
            lane = lax.broadcasted_iota(jnp.int32, (ROWS, LANES), 1)
            tiles = []
            for k in range(width):
                column = jnp.broadcast_to(index[:, k : k + 1], (ROWS, LANES))
                tiles.append(
                    jnp.where((column & (LANES - 1)) == lane, column >> 7, -1).astype(F32).astype(BF16)
                )
            one = jnp.ones((ROWS, LANES), BF16)
            zero = jnp.zeros((ROWS, LANES), BF16)
            tile = 0
            for out_ref in out_refs:
                for at in range(out_ref.shape[1] // LANES):
                    total = jnp.where(tiles[0] == tile, one, zero)
                    for k in range(1, width):
                        total = total + jnp.where(tiles[k] == tile, one, zero)
                    out_ref[pl.ds(first, ROWS), at * LANES : (at + 1) * LANES] = total
                    tile += 1

    @pl.when(step < single_blocks)
    def _():
        fill(1)

    @pl.when(step >= single_blocks)
    def _():
        fill(terms)


def count_matrices(index, singles, widths, terms):
    nodes, padded = index.shape
    block_rows = 64
    return pl.pallas_call(
        functools.partial(
            count_kernel, single_blocks=singles // block_rows, block_rows=block_rows, terms=terms
        ),
        grid=(nodes // block_rows,),
        in_specs=[pl.BlockSpec((block_rows, padded), lambda i: (i, 0))],
        out_specs=[pl.BlockSpec((block_rows, w), lambda i: (i, 0)) for w in widths],
        out_shape=[jax.ShapeDtypeStruct((nodes, w), BF16) for w in widths],
        cost_estimate=pl.CostEstimate(
            flops=nodes * sum(widths) * terms * 2, bytes_accessed=nodes * sum(widths) * 2, transcendentals=0
        ),
        name="count_matrices",
    )(index)


def node_index(seed_source, hop1_source, hop2_source, terms):
    def pad(v):
        return jnp.pad(v, ((0, 0), (0, terms - v.shape[1])), constant_values=-1)

    hop1 = hop1_source.reshape(-1)
    return jnp.concatenate(
        [
            pad(seed_source.reshape(-1, 1)),
            pad(hop1.reshape(-1, 1)),
            pad(hop1.reshape(-1, K2)),
            pad(hop2_source.reshape(-1, K1)),
        ],
        0,
    )


def ring(axis_size, shift):
    return [(i, (i + shift) % axis_size) for i in range(axis_size)]


def body(
    hot_table,
    cold_table,
    seed_source,
    hop1_source,
    hop2_source,
    cold_ask,
    cotangent,
    w1_self,
    w1_neigh,
    w2_self,
    w2_neigh,
    *,
    owners,
    planes,
):
    width = hot_table.shape[1]
    hidden_width = w1_self.shape[1]
    seeds_count = seed_source.shape[1]
    hop1_count = hop1_source.shape[1]
    nodes = seeds_count + hop1_count
    half = hot_table.shape[0]
    hot_rows = 2 * half
    cap = cold_ask.shape[2]
    part = cap // CHUNKS
    core = lax.axis_index("clique")

    hot_other = lax.ppermute(hot_table, "clique", [(0, 1), (1, 0)])
    asked = lax.all_to_all(cold_ask[0], "hst", split_axis=0, concat_axis=0, tiled=True)
    cold_parts = []
    for j in range(CHUNKS):
        rows = asked[:, j * part : (j + 1) * part].reshape(-1)
        picked = cold_table.at[rows].get(mode="promise_in_bounds")
        cold_parts.append(lax.all_to_all(picked, "hst", split_axis=0, concat_axis=0, tiled=True))

    index = node_index(seed_source, hop1_source, hop2_source, 16)
    offset = index - hot_rows
    owner, slot = offset // cap, offset % cap
    cold_index = hot_rows + (slot // part) * (owners * part) + owner * part + slot % part
    hot_index = (index + half * core) & (hot_rows - 1)
    index = jnp.where(index < 0, -1, jnp.where(index < hot_rows, hot_index, cold_index))
    counts = count_matrices(index, nodes, [half, half] + [owners * part] * CHUNKS, K1)
    sums = matmul(counts[0], hot_table) + matmul(counts[1], hot_other)
    for j in range(CHUNKS):
        sums = sums + matmul(counts[2 + j], cold_parts[j])

    grad_seed = inner_cols(cotangent, w2_self)
    grad_mean = inner_cols(cotangent, w2_neigh) / K2
    grad_hop = jnp.broadcast_to(grad_mean[:, None, :], (seeds_count, K2, hidden_width)).reshape(
        seeds_count * K2, hidden_width
    )
    grad_hidden = jnp.concatenate([grad_seed, grad_hop], 0)

    level_in = sums[:nodes].astype(BF16)
    level_mean = jnp.concatenate(
        [
            (sums[nodes : nodes + seeds_count] / K2).astype(BF16),
            (sums[nodes + seeds_count :] / K1).astype(BF16),
        ],
        0,
    )
    pre = matmul(level_in, w1_self) + matmul(level_mean, w1_neigh)
    hidden = jnp.maximum(pre, 0.0).astype(BF16)
    grad_pre = jnp.where(pre > 0, grad_hidden, 0.0).astype(BF16)
    hidden_seed = hidden[:seeds_count]
    pool = (
        lax.broadcasted_iota(jnp.int32, (seeds_count, hop1_count), 1) // K2
        == lax.broadcasted_iota(jnp.int32, (seeds_count, hop1_count), 0)
    ).astype(BF16)
    hidden_mean = (matmul(pool, hidden[seeds_count:]) / K2).astype(BF16)
    embedding = (matmul(hidden_seed, w2_self) + matmul(hidden_mean, w2_neigh)).astype(BF16)

    pairs = ((level_in, grad_pre), (level_mean, grad_pre), (hidden_seed, cotangent), (hidden_mean, cotangent))

    def terms_of(which):
        first = which * (width // 2)
        return jnp.concatenate(
            [
                inner_rows(lax.dynamic_slice_in_dim(left, first, width // 2, 1), right)[None]
                for left, right in pairs
            ],
            0,
        )

    given = lax.ppermute(terms_of(1 - core).astype(BF16), "clique", [(0, 1), (1, 0)])
    kept = (terms_of(core) + given.astype(F32)).astype(BF16)
    block = width // 2 // owners
    kept = kept.reshape(len(pairs), owners, block, hidden_width).transpose(1, 0, 2, 3)
    shares = lax.all_to_all(kept, "hst", split_axis=0, concat_axis=0, tiled=True)
    share = jnp.sum(shares, axis=0, dtype=F32).astype(BF16)
    after, before, across = (lax.ppermute(share, "dp", ring(planes, s)) for s in (1, 3, 2))
    total = (share.astype(F32) + across.astype(F32)) + (after.astype(F32) + before.astype(F32))
    return (embedding, total[0], total[1], total[2], total[3])


def solution(mesh):
    rows = P(("clique", "dp", "hst"), None)
    in_specs = (
        P("clique", None),
        P("hst", None),
        rows,
        rows,
        rows,
        P(("clique", "dp", "hst"), None, None),
        rows,
        P(),
        P(),
        P(),
        P(),
    )
    shares = P(("clique", "hst"), None)
    out_specs = (rows, shares, shares, shares, shares)
    run = functools.partial(body, owners=mesh.shape["hst"], planes=mesh.shape["dp"])
    return jax.shard_map(run, mesh=mesh, in_specs=in_specs, out_specs=out_specs, check_vma=False)
```

```python
import functools

import jax
import jax.numpy as jnp
from jax import lax
from jax.experimental import pallas as pl
from jax.experimental.pallas import tpu as pltpu
from jax.sharding import PartitionSpec as P

K2 = 10
K1 = 15
LANES = 128
ROWS = 16


BF16 = jnp.bfloat16
F32 = jnp.float32


def matmul(left, right):
    return jnp.dot(left, right, preferred_element_type=F32)


def inner_rows(left, right):
    return lax.dot_general(left, right, (((0,), (0,)), ((), ())), preferred_element_type=F32)


def inner_cols(left, right):
    return lax.dot_general(left, right, (((1,), (1,)), ((), ())), preferred_element_type=F32)


def count_kernel(index_ref, *out_refs, single_blocks, block_rows, terms):
    step = pl.program_id(0)
    tiles = [(ref, at) for ref in out_refs for at in range(ref.shape[1] // LANES)]

    def fill(width):
        @pl.loop(0, block_rows // ROWS)
        def _(group):
            first = pl.multiple_of(group * ROWS, ROWS)
            index = index_ref[pl.ds(first, ROWS), :]
            lane = lax.broadcasted_iota(jnp.int32, (ROWS, LANES), 1)
            words, units = [], []
            for k in range(width):
                column = jnp.broadcast_to(index[:, k : k + 1], (ROWS, LANES))
                tile = column >> 7
                words.append(tile >> 3)
                unit = lax.shift_left(jnp.ones_like(tile), (tile & 7) << 2)
                units.append(jnp.where((column & (LANES - 1)) == lane, unit, 0))
            for word in range(len(tiles) // 8):
                packed = jnp.where(words[0] == word, units[0], 0)
                for k in range(1, width):
                    packed = packed + jnp.where(words[k] == word, units[k], 0)
                for nibble in range(8):
                    ref, at = tiles[word * 8 + nibble]
                    count = lax.shift_right_logical(packed, 4 * nibble) & 15
                    ref[pl.ds(first, ROWS), at * LANES : (at + 1) * LANES] = count.astype(F32).astype(BF16)

    @pl.when(step < single_blocks)
    def _():
        fill(1)

    @pl.when(step >= single_blocks)
    def _():
        fill(terms)


def count_matrices(index, singles, widths, terms):
    nodes, padded = index.shape
    block_rows = 64
    return pl.pallas_call(
        functools.partial(
            count_kernel, single_blocks=singles // block_rows, block_rows=block_rows, terms=terms
        ),
        grid=(nodes // block_rows,),
        in_specs=[pl.BlockSpec((block_rows, padded), lambda i: (i, 0))],
        out_specs=[pl.BlockSpec((block_rows, w), lambda i: (i, 0)) for w in widths],
        out_shape=[jax.ShapeDtypeStruct((nodes, w), BF16) for w in widths],
        cost_estimate=pl.CostEstimate(
            flops=nodes * sum(widths) * terms * 2, bytes_accessed=nodes * sum(widths) * 2, transcendentals=0
        ),
        name="count_matrices",
    )(index)


def add_kernel(sums_ref, *refs):
    terms = len(refs) // 2
    span = 256

    @pl.loop(0, sums_ref.shape[1] // span)
    def _(step):
        columns = pl.ds(pl.multiple_of(step * span, span), span)
        total = sums_ref[:, columns]
        for k in range(terms):
            total = total + jnp.dot(refs[k][...], refs[terms + k][:, columns], preferred_element_type=F32)
        refs[-1][:, columns] = total


def add_products(sums, counts, rows):
    nodes, width = sums.shape
    block_rows = 128
    deep = sum(r.shape[0] for r in rows)
    return pl.pallas_call(
        add_kernel,
        grid=(nodes // block_rows,),
        in_specs=[pl.BlockSpec((block_rows, width), lambda i: (i, 0))]
        + [pl.BlockSpec((block_rows, c.shape[1]), lambda i: (i, 0)) for c in counts]
        + [pl.BlockSpec(r.shape, lambda i: (0, 0)) for r in rows],
        out_specs=pl.BlockSpec((block_rows, width), lambda i: (i, 0)),
        out_shape=jax.ShapeDtypeStruct((nodes, width), F32),
        input_output_aliases={0: 0},
        cost_estimate=pl.CostEstimate(
            flops=2 * nodes * width * deep,
            bytes_accessed=8 * nodes * width + 2 * deep * (nodes + width),
            transcendentals=0,
        ),
        name="add_products",
    )(sums, *counts, *rows)


def node_index(seed_source, hop1_source, hop2_source, terms):
    def pad(v):
        return jnp.pad(v, ((0, 0), (0, terms - v.shape[1])), constant_values=-1)

    hop1 = hop1_source.reshape(-1)
    return jnp.concatenate(
        [
            pad(seed_source.reshape(-1, 1)),
            pad(hop1.reshape(-1, 1)),
            pad(hop1.reshape(-1, K2)),
            pad(hop2_source.reshape(-1, K1)),
        ],
        0,
    )


def moved(place, offset, side):
    return ((place // side + offset // side) % side) * side + (place + offset) % side


def hops(offset, side):
    return sum(min(step, side - step) for step in (offset // side, offset % side))


def ring(axis_size, shift):
    return [(i, (i + shift) % axis_size) for i in range(axis_size)]


def body(
    hot_table,
    cold_table,
    seed_source,
    hop1_source,
    hop2_source,
    cold_ask,
    cotangent,
    w1_self,
    w1_neigh,
    w2_self,
    w2_neigh,
    *,
    owners,
    planes,
    side,
):
    width = hot_table.shape[1]
    hidden_width = w1_self.shape[1]
    seeds_count = seed_source.shape[1]
    hop1_count = hop1_source.shape[1]
    nodes = seeds_count + hop1_count
    half = hot_table.shape[0]
    hot_rows = 2 * half
    cap = cold_ask.shape[2]
    core = lax.axis_index("clique")
    here = lax.axis_index("hst")

    hot_other = lax.ppermute(hot_table, "clique", [(0, 1), (1, 0)])
    asked = lax.all_to_all(cold_ask[0], "hst", split_axis=0, concat_axis=0, tiled=True)
    offset = jnp.arange(owners)
    asked = asked.at[moved(here, offset, side)].get(mode="promise_in_bounds")
    order = sorted(range(1, owners), key=lambda o: -hops(o, side))
    picked = None
    cold_rows = {}
    for o in order:
        rows = asked[o]
        if picked is not None:
            rows, picked = lax.optimization_barrier((rows, picked))
        picked = cold_table.at[rows].get(mode="promise_in_bounds")
        if o != order[-1]:
            cold_rows[o] = lax.ppermute(picked, "hst", [(i, moved(i, o, side)) for i in range(owners)])
    cold_rows[0] = cold_table.at[asked[0]].get(mode="promise_in_bounds")

    index = node_index(seed_source, hop1_source, hop2_source, 16)
    spot = index - hot_rows
    owner = spot // cap
    apart = ((here // side - owner // side) % side) * side + (here - owner) % side
    cold_index = hot_rows + apart * cap + spot % cap
    hot_index = (index + half * core) & (hot_rows - 1)
    index = jnp.where(index < 0, -1, jnp.where(index < hot_rows, hot_index, cold_index))
    counts = count_matrices(index, nodes, [half, half] + [cap] * owners, K1)
    hot_counts, cotangent, picked = lax.optimization_barrier((counts[:2], cotangent, picked))
    cold_rows[order[-1]] = lax.ppermute(
        picked, "hst", [(i, moved(i, order[-1], side)) for i in range(owners)]
    )
    sums = matmul(hot_counts[0], hot_table) + matmul(hot_counts[1], hot_other)
    sequence = [0] + order
    for first, last in ((0, 5), (5, 9), (9, 12), (12, 14), (14, 16)):
        group = sequence[first:last]
        sums = add_products(sums, [counts[2 + o] for o in group], [cold_rows[o] for o in group])

    grad_seed = inner_cols(cotangent, w2_self)
    grad_mean = inner_cols(cotangent, w2_neigh) / K2
    grad_hop = jnp.broadcast_to(grad_mean[:, None, :], (seeds_count, K2, hidden_width)).reshape(
        seeds_count * K2, hidden_width
    )
    grad_hidden = jnp.concatenate([grad_seed, grad_hop], 0)

    level_in = sums[:nodes].astype(BF16)
    level_mean = jnp.concatenate(
        [
            (sums[nodes : nodes + seeds_count] / K2).astype(BF16),
            (sums[nodes + seeds_count :] / K1).astype(BF16),
        ],
        0,
    )
    pre = matmul(level_in, w1_self) + matmul(level_mean, w1_neigh)
    hidden = jnp.maximum(pre, 0.0).astype(BF16)
    grad_pre = jnp.where(pre > 0, grad_hidden, 0.0).astype(BF16)
    hidden_seed = hidden[:seeds_count]
    pool = (
        lax.broadcasted_iota(jnp.int32, (seeds_count, hop1_count), 1) // K2
        == lax.broadcasted_iota(jnp.int32, (seeds_count, hop1_count), 0)
    ).astype(BF16)
    hidden_mean = (matmul(pool, hidden[seeds_count:]) / K2).astype(BF16)
    embedding = (matmul(hidden_seed, w2_self) + matmul(hidden_mean, w2_neigh)).astype(BF16)

    pairs = ((level_in, grad_pre), (level_mean, grad_pre), (hidden_seed, cotangent), (hidden_mean, cotangent))

    def terms_of(which):
        first = which * (width // 2)
        return [
            inner_rows(lax.dynamic_slice_in_dim(left, first, width // 2, 1), right) for left, right in pairs
        ]

    given = [lax.ppermute(t.astype(BF16), "clique", [(0, 1), (1, 0)]) for t in terms_of(1 - core)]
    block = width // 2 // owners
    kept = jnp.stack(
        [
            (own + other.astype(F32)).astype(BF16).reshape(owners, block, hidden_width)
            for own, other in zip(terms_of(core), given)
        ],
        1,
    )
    shares = lax.all_to_all(kept, "hst", split_axis=0, concat_axis=0, tiled=True)
    share = jnp.sum(shares, axis=0, dtype=F32).astype(BF16)
    after, before, across = (lax.ppermute(share, "dp", ring(planes, s)) for s in (1, 3, 2))
    total = (share.astype(F32) + across.astype(F32)) + (after.astype(F32) + before.astype(F32))
    return (embedding, total[0], total[1], total[2], total[3])


def solution(mesh):
    rows = P(("clique", "dp", "hst"), None)
    in_specs = (
        P("clique", None),
        P("hst", None),
        rows,
        rows,
        rows,
        P(("clique", "dp", "hst"), None, None),
        rows,
        P(),
        P(),
        P(),
        P(),
    )
    shares = P(("clique", "hst"), None)
    out_specs = (rows, shares, shares, shares, shares)
    run = functools.partial(body, owners=mesh.shape["hst"], planes=mesh.shape["dp"], side=int(mesh.shape["hst"] ** 0.5))
    return jax.shard_map(run, mesh=mesh, in_specs=in_specs, out_specs=out_specs, check_vma=False)
```
